32 devices in a mesh: segment: 4 (over y, x), tile: 8 (over z, core).
Axes of the slice: x: 2, y: 2, z: 4, core: 2. Of those that a mesh axis runs over, the one named last changes fastest.
Arguments:
- raw_frames: bfloat16 [32, 1280, 1280], P(('segment', 'tile')), may hold values from -6 to 6
- dark_frame: bfloat16 [1280, 1280], replicated, may hold values from -2.5 to 2.5
- flat_field: bfloat16 [1280, 1280], replicated, may hold values from 0.25 to 1.75
- seeing: float32 [32, 64], P(None, 'tile'), may hold values from 0.1 to 10
- anchors: int32 [64, 2], replicated, may hold values from 0 to 1023, as said below
- taper: int32 [64], replicated, may hold values from 16 to 64
Outputs:
- power: float32 [64, 256, 256], P('tile', 'segment')
- cross: float32 [64, 4, 256, 256], P('tile', None, 'segment')
The draws below stay inside these ranges and needn't reach their ends.
Inputs may be any that keep to these rules, and one draw needn't show every extreme that they name: `anchors`: the subfield g = 8 i + j has anchor (128 i + a, 128 j + b) with a and b below 128.
All inputs are finite; a program needn't handle non-finite values.
Results may differ from the reference program's by a relative error of at most 0.013.
Values may be sent and summed in bfloat16 or wider, within the bound.
No kernel may reach another device: no remote copies, remote signals or barrier semaphores. Data moves between devices by JAX's collectives and lax.ppermute only.
A program may use at most 192 MiB of HBM per device.

```python
import math
import jax
import jax.numpy as jnp
from jax import lax

S = 256
GRID = 8
STRIDE = 128
IMG = 1280
SUBFIELDS = 64
FRAMES = 32


def draw_anchors(key, part):
    jitter = jax.random.randint(key, (GRID, GRID, 2), 0, STRIDE)
    jitter = jitter.at[0, 0].set(0).at[GRID - 1, GRID - 1].set(STRIDE - 1)
    rows = jnp.broadcast_to(jnp.arange(GRID, dtype=jnp.int32)[:, None], (GRID, GRID))
    cols = jnp.broadcast_to(jnp.arange(GRID, dtype=jnp.int32)[None, :], (GRID, GRID))
    base = jnp.stack([rows, cols], axis=-1) * STRIDE
    return (base + jitter).reshape(GRID * GRID, 2).astype(jnp.int32)


def with_ends(result, stream_key, low, top_value):
    longest = result.shape.index(max(result.shape))
    spots = []
    for shift in (0, 1):
        where = [jax.random.randint(jax.random.fold_in(stream_key, axis), (), 0, length) for axis, length in enumerate(result.shape)]
        where[longest] = (where[longest] + shift) % result.shape[longest]
        spots.append(tuple(where))
    return result.at[spots[0]].set(low).at[spots[1]].set(top_value)


def steps_of(key, dims, pieces, smallest, top_value):
    def one(dim, blocks):
        heights = jax.random.uniform(jax.random.fold_in(jax.random.fold_in(key, 6), dim), (blocks,), jnp.float32, smallest / len(pieces), top_value / len(pieces))
        return jnp.repeat(jnp.exp(heights), dims[dim] // blocks).reshape((-1,) + (1,) * (len(dims) - dim - 1))

    loudness = one(*pieces[0])
    for cut in pieces[1:]:
        loudness = loudness * one(*cut)
    return loudness


def gaussian(rng, extent, spread, bound, shards=(), held_as=jnp.bfloat16):
    entries = jax.random.normal(rng, extent, jnp.float32) * spread
    if len(shards) > 0:
        entries = steps_of(rng, extent, shards, -0.22, 0.18) * entries
    return jnp.clip(entries, min=-bound, max=bound).astype(held_as)


def setup_inputs(seed: int = 0) -> dict:
    seeds = jax.random.split(jax.random.key(seed), 7)
    return {
        "raw_frames": gaussian(seeds[0], (FRAMES, IMG, IMG), 1.0, 6.0, ((0, 32),)),
        "dark_frame": gaussian(seeds[1], (IMG, IMG), 0.3, 2.5),
        "flat_field": jnp.clip(1.0 + 0.15 * jax.random.normal(seeds[2], (IMG, IMG), jnp.float32), 0.25, 1.75).astype(jnp.bfloat16),
        "seeing": jnp.clip(jnp.exp(math.log(10.0) - 4.6051702 * jax.random.uniform(seeds[3], (FRAMES, SUBFIELDS), jnp.float32) ** steps_of(seeds[3], (FRAMES, SUBFIELDS), ((1, 8),), -0.2, 0.2)), 0.1, 10.0),
        "anchors": draw_anchors(jax.random.fold_in(seeds[6], 71), 0),
        "taper": with_ends(jax.random.randint(seeds[5], (SUBFIELDS,), S // 16, S // 4 + 1), jax.random.fold_in(seeds[5], 1), S // 16, (S // 4 + 1) - 1).astype(jnp.int32),
    }


def ramp_rows(taper):
    place = jnp.arange(S, dtype=jnp.float32)
    width = taper.astype(jnp.float32)
    left = jnp.where(place < width, 0.5 - 0.5 * jnp.cos(jnp.pi * (place + 0.5) / width), 1.0)
    return left * left[::-1]

def reference(raw_frames, dark_frame, flat_field, seeing, anchors, taper):
    scale = jnp.sqrt(jnp.float32(S))

    def one_field(index):
        anchor = anchors[index]
        start = jnp.zeros((), jnp.int32)
        piece = lax.dynamic_slice(raw_frames, (start, anchor[0], anchor[1]), (FRAMES, S, S)).astype(jnp.float32)
        dark_piece = lax.dynamic_slice(dark_frame, (anchor[0], anchor[1]), (S, S)).astype(jnp.float32)
        flat_piece = lax.dynamic_slice(flat_field, (anchor[0], anchor[1]), (S, S)).astype(jnp.float32)
        cal = (piece - dark_piece[None]) / flat_piece[None]
        centered = cal - lax.optimization_barrier(jnp.mean(cal, axis=(1, 2), keepdims=True))
        ramp = ramp_rows(taper[index])
        sub = (centered * (ramp[:, None] * ramp[None, :])[None]).astype(jnp.bfloat16)
        first = jnp.fft.fft(sub.astype(jnp.float32), axis=2) / scale
        real_half = lax.optimization_barrier(jnp.real(first).astype(jnp.bfloat16)).astype(jnp.float32)
        imag_half = lax.optimization_barrier(jnp.imag(first).astype(jnp.bfloat16)).astype(jnp.float32)
        second = jnp.fft.fft(real_half + 1j * imag_half, axis=1) / scale
        real_part = jnp.real(second).astype(jnp.float32)
        imag_part = jnp.imag(second).astype(jnp.float32)
        weights = seeing[:, index]
        weight_sum = jnp.sum(weights)
        wgt = weights[:, None, None]
        power_sum = lax.optimization_barrier(jnp.sum(wgt * (real_part * real_part + imag_part * imag_part), axis=0))
        real_u = jnp.roll(real_part, -1, axis=1)
        imag_u = jnp.roll(imag_part, -1, axis=1)
        real_v = jnp.roll(real_part, -1, axis=2)
        imag_v = jnp.roll(imag_part, -1, axis=2)
        cross_sum = jnp.stack([lax.optimization_barrier(jnp.sum(wgt * (real_part * real_u + imag_part * imag_u), axis=0)), lax.optimization_barrier(jnp.sum(wgt * (imag_part * real_u - real_part * imag_u), axis=0)), lax.optimization_barrier(jnp.sum(wgt * (real_part * real_v + imag_part * imag_v), axis=0)), lax.optimization_barrier(jnp.sum(wgt * (imag_part * real_v - real_part * imag_v), axis=0))], axis=0)
        return (power_sum / weight_sum, cross_sum / weight_sum)
    power, cross = lax.map(one_field, jnp.arange(SUBFIELDS, dtype=jnp.int32))
    return (power, cross)
```

```python
import math

import jax
import jax.numpy as jnp
import numpy as np
from jax import lax
from jax.experimental import pallas as pl
from jax.experimental.pallas import tpu as pltpu
from jax.sharding import PartitionSpec as P

S = 256
HALF = 128
WIN = 384
ROWS = 656
BF = jnp.bfloat16
F32 = jnp.float32


def ramp_at(place, width):
    def side(x):
        return jnp.where(x < width, 0.5 - 0.5 * jnp.cos(jnp.pi * (x + 0.5) / width), 1.0)

    inside = (place >= 0) & (place < S)
    return jnp.where(inside, side(place) * side(S - 1.0 - place), 0.0)


def half_tables():
    def angle(n, m):
        return 2.0 * np.pi * ((np.arange(n)[:, None] * np.arange(m)[None, :]) % S) / S

    first = angle(WIN, S)
    second = angle(HALF + 8, S)
    t = np.concatenate([np.cos(first), -np.sin(first)], axis=1) / 16.0
    w = np.concatenate([np.cos(second), np.sin(second)], axis=0) / 16.0
    return jnp.asarray(t.astype(np.float32)).astype(BF), jnp.asarray(w.astype(np.float32)).astype(BF)


def spectra_body(n_frames, rows, wts, wa, wb, da, db, fa, fb, rx, ry, mk, t_ref, w_ref, keep, give, cal, sub, z, y):
    k = pl.program_id(0)
    for h, (w, d, f) in enumerate(((wa, da, fa), (wb, db, fb))):

        def calibrate(step, carry, h=h, w=w, d=d, f=f):
            at = pl.multiple_of(step * 16, 16)
            inverse = 1.0 / f[pl.ds(at, 16), :].astype(F32)
            dark = d[pl.ds(at, 16), :].astype(F32)
            for fr in range(n_frames):
                value = (w[fr, pl.ds(at, 16), :].astype(F32) - dark) * inverse
                for n in range(4):
                    cal[fr, n, pl.ds(h * S + at, 16), :] = value[:, n * HALF : (n + 1) * HALF]
            return carry

        lax.fori_loop(0, S // 16, calibrate, 0)

    def one(q, carry):
        which, col = q // 2, q % 2
        start = rows[k * 4 + q]
        rowr = ry[q, 0:1, :]
        mask = mk[q, 0:1, :]
        for fr in range(n_frames):
            mean = jnp.zeros((1, 1), F32)
            for m in range(3):
                total = cal[fr, col + m, pl.ds(start, 8), :]
                for n in range(1, S // 8):
                    total = total + cal[fr, col + m, pl.ds(start + 8 * n, 8), :]
                weighed = jnp.sum(total * mask[:, m * HALF : (m + 1) * HALF], axis=0, keepdims=True)
                mean = mean + jnp.sum(weighed, axis=1, keepdims=True)
            for n in range(S // 16):
                col_r = rx[q, 16 * n : 16 * n + 16, :]
                for m in range(3):
                    c = cal[fr, col + m, pl.ds(start + 16 * n, 16), :]
                    ramp = col_r * rowr[:, m * HALF : (m + 1) * HALF]
                    sub[fr, 16 * n : 16 * n + 16, m * HALF : (m + 1) * HALF] = ((c - mean) * ramp).astype(BF)
        for fr in range(n_frames):
            z[fr] = jnp.dot(sub[fr], t_ref[...], preferred_element_type=F32).astype(BF)
        for fr in range(n_frames):
            both = jnp.dot(w_ref[...], z[fr], preferred_element_type=F32)
            for n in range(4):
                y[fr, n] = both[:, n * HALF : (n + 1) * HALF]

        def spec_rows(fr, at, n):
            a = [y[fr, m, pl.ds(at, n), :] for m in range(4)]
            b = [y[fr, m, pl.ds(at + HALF + 8, n), :] for m in range(4)]
            re = jnp.concatenate([a[0] + b[2], a[1] + b[3]], axis=1)
            return re, jnp.concatenate([a[2] - b[0], a[3] - b[1]], axis=1)

        def weighted(at, n, shift_u):
            acc = None
            for fr in range(n_frames):
                wgt = wts[(k * 4 + q) * n_frames + fr]
                re, im = spec_rows(fr, at, n)
                wre, wim = re * wgt, im * wgt
                re_v, im_v = pltpu.roll(re, S - 1, axis=1), pltpu.roll(im, S - 1, axis=1)
                terms = [wre * re + wim * im]
                if shift_u:
                    re_u, im_u = spec_rows(fr, at + 1, n)
                    terms += [wre * re_u + wim * im_u, wim * re_u - wre * im_u]
                terms += [wre * re_v + wim * im_v, wim * re_v - wre * im_v]
                acc = terms if acc is None else [p + r for p, r in zip(acc, terms)]
            return acc

        def store(at, value):
            @pl.when(which == 0)
            def _():
                keep[0, col, pl.ds(at, 16), :] = value

            @pl.when(which == 1)
            def _():
                give[0, col, pl.ds(at, 16), :] = value

        def block(r, c2):
            at = pl.multiple_of(r * 16, 16)
            acc = weighted(at, 16, True)
            for n, value in enumerate(acc):
                store(pl.multiple_of(n * HALF + at, 16), value.astype(BF))
            return c2

        lax.fori_loop(0, HALF // 16, block, 0)
        last = [jnp.broadcast_to(v[0:1, :], (16, S)) for v in weighted(HALF, 8, False)]
        line = lax.broadcasted_iota(jnp.int32, (16, S), 0)
        tail = jnp.where(line == 0, last[0], jnp.where(line == 1, last[1], jnp.where(line == 2, last[2], 0.0)))
        store(5 * HALF, tail.astype(BF))
        return carry

    lax.fori_loop(0, 4, one, 0)


def spectra(rows, wts, win, dark, flat, rx, ry, mk, t, w):
    n_frames, height, width = win.shape
    steps = height // S - 1
    vm = pltpu.VMEM

    def pair(shape, lead):
        return [
            pl.BlockSpec(shape, lambda k, r, s, d=d: (0,) * lead + (k + d, 0)) for d in (0, 1)
        ]

    def whole(shape):
        return pl.BlockSpec(shape, lambda k, r, s: (0,) * len(shape))

    def per_step(shape):
        return pl.BlockSpec(shape, lambda k, r, s: (k,) + (0,) * (len(shape) - 1))

    out = jax.ShapeDtypeStruct((steps, 2, ROWS, S), BF)
    return pl.pallas_call(
        lambda *refs: spectra_body(n_frames, *refs),
        out_shape=(out, out),
        grid_spec=pltpu.PrefetchScalarGridSpec(
            num_scalar_prefetch=2,
            grid=(steps,),
            in_specs=pair((n_frames, S, width), 1)
            + pair((S, width), 0)
            + pair((S, width), 0)
            + [per_step((4, S, HALF)), per_step((4, 8, WIN)), per_step((4, 8, WIN)), whole(t.shape), whole(w.shape)],
            out_specs=(per_step((1, 2, ROWS, S)), per_step((1, 2, ROWS, S))),
            scratch_shapes=[
                vm((n_frames, width // HALF, 2 * S, HALF), F32),
                vm((n_frames, S, WIN), BF),
                vm((n_frames, S, 2 * S), BF),
                vm((n_frames, 4, 2 * HALF + 16, HALF), F32),
            ],
        ),
        compiler_params=pltpu.CompilerParams(dimension_semantics=("arbitrary",), vmem_limit_bytes=56 << 20),
        cost_estimate=pl.CostEstimate(flops=16_000_000_000, bytes_accessed=20_000_000, transcendentals=0),
        name="spectra",
    )(rows, wts, win, win, dark, dark, flat, flat, rx, ry, mk, t, w)


def finish_body(scal, x, flip, rot, lines, power, cross):
    def moved(n, m, at):
        right = jnp.dot(x[n, m], at, preferred_element_type=F32).astype(BF)
        return jnp.dot(lines[...], right, preferred_element_type=F32)

    n = pl.program_id(0)
    for m in range(2):
        g = n * 2 + m
        inv, cb, sb = scal[g * 3], scal[g * 3 + 1], scal[g * 3 + 2]
        got = [jnp.dot(x[0, m, p], (flip if p < 3 else rot)[...], preferred_element_type=F32).astype(BF) for p in range(5)]
        got = [jnp.dot(lines[...], v, preferred_element_type=F32) for v in got]
        power[m] = got[0] * inv
        cross[m, 0] = got[1] * inv
        cross[m, 1] = got[2] * inv
        cross[m, 2] = (got[3] * cb + got[4] * sb) * inv
        cross[m, 3] = (got[4] * cb - got[3] * sb) * inv


def finish(scal, x, flip, rot, lines):
    n_seg, per, _, height, _ = x.shape
    count = n_seg * per

    def whole(a):
        return pl.BlockSpec(a.shape, lambda k, s: (0,) * a.ndim)

    return pl.pallas_call(
        finish_body,
        out_shape=(
            jax.ShapeDtypeStruct((count, height, S), F32),
            jax.ShapeDtypeStruct((count, 4, height, S), F32),
        ),
        grid_spec=pltpu.PrefetchScalarGridSpec(
            num_scalar_prefetch=1,
            grid=(n_seg,),
            in_specs=[
                pl.BlockSpec((1, per, 5, height, S), lambda k, s: (k, 0, 0, 0, 0)),
                whole(flip),
                whole(rot),
                whole(lines),
            ],
            out_specs=(
                pl.BlockSpec((per, height, S), lambda k, s: (k, 0, 0)),
                pl.BlockSpec((per, 4, height, S), lambda k, s: (k, 0, 0, 0)),
            ),
        ),
        compiler_params=pltpu.CompilerParams(dimension_semantics=("arbitrary",)),
        cost_estimate=pl.CostEstimate(flops=400_000_000, bytes_accessed=4_000_000, transcendentals=0),
        name="finish",
    )(scal, x, flip, rot, lines)


def pick(array, index, axis):
    return lax.dynamic_index_in_dim(array, index, axis, keepdims=False)


def planes(raw_frames, dark_frame, flat_field, seeing, anchors, taper):
    seg = lax.axis_index("segment")
    tile = lax.axis_index("tile")
    z, core = tile // 2, tile % 2

    send = jnp.stack([raw_frames[0, :, S * d : S * d + 2 * S] for d in range(4)])
    win = lax.all_to_all(send, "segment", split_axis=0, concat_axis=0, tiled=True)

    by_tile = seeing.reshape(4, 8, 8).transpose(1, 0, 2)
    weights = lax.all_to_all(by_tile, "tile", split_axis=0, concat_axis=0, tiled=True)

    def mine(grid_array):
        cols = lax.dynamic_slice_in_dim(grid_array, 2 * seg, 2, 1)
        cols = cols.reshape((4, 2) + cols.shape[1:])
        return jnp.where(core == 0, cols, cols[:, ::-1])

    wts = mine(weights.transpose(0, 2, 1)).reshape(-1)
    spots = anchors.reshape(8, 8, 2)
    offset = spots - 128 * jnp.stack(jnp.meshgrid(jnp.arange(8), jnp.arange(8), indexing="ij"), -1)
    rows = (mine(spots[..., 0]) - S * jnp.arange(4)[:, None, None]).reshape(-1)
    shift = mine(offset[..., 1]).reshape(-1).astype(F32)
    width = mine(taper.reshape(8, 8)).reshape(-1).astype(F32)
    x = jnp.arange(S, dtype=F32)
    rx = jnp.broadcast_to(ramp_at(x[None, :], width[:, None])[:, :, None], (16, S, HALF))
    place = jnp.arange(WIN, dtype=F32)[None, :] - shift[:, None]
    ry = jnp.broadcast_to(ramp_at(place, width[:, None])[:, None, :], (16, 8, WIN))
    inside = jnp.where((place >= 0) & (place < S), 1.0 / (S * S), 0.0)
    mk = jnp.broadcast_to(inside[:, None, :], (16, 8, WIN))
    dark = lax.dynamic_slice_in_dim(dark_frame, S * seg, 2 * S, 1)
    flat = lax.dynamic_slice_in_dim(flat_field, S * seg, 2 * S, 1)

    t, w = half_tables()
    keep, give = spectra(rows.astype(jnp.int32), wts, win, dark, flat, rx, ry, mk, t, w)

    other = lax.ppermute(give, "tile", [(n, n ^ 1) for n in range(8)])

    def own(index):
        index = jnp.clip(index, 0, 3)
        return pick(keep, index, 0).astype(F32) + pick(other, index, 0).astype(F32)

    up = down = None
    for k in range(3):
        up_send = own(3 + z - k)
        down_send = own(z - 3 + k)
        if k > 0:
            up_send = up_send + up.astype(F32)
            down_send = down_send + down.astype(F32)
        lower = [n for n in range(8) if n // 2 <= min(k, 2)]
        upper = [n for n in range(8) if 3 - n // 2 <= min(k, 2)]
        up = lax.ppermute(up_send.astype(BF), "tile", [(n, n + 2) for n in lower])
        down = lax.ppermute(down_send.astype(BF), "tile", [(n, n - 2) for n in upper])
    total = (own(z) + up.astype(F32) + down.astype(F32)).astype(BF)

    body = total[:, : 5 * HALF].reshape(2, 5, HALF, S)
    row128 = total[:, 5 * HALF : 5 * HALF + 3]
    extra = jnp.stack([row128[:, 0], row128[:, 0], row128[:, 0], row128[:, 1], row128[:, 2]], axis=1)[:, :, None]
    later = jnp.concatenate([body[:, :, 1:], extra], axis=2)
    shifted = jnp.concatenate([later[:, :1], body[:, 1:3], later[:, 3:]], axis=1)
    deal = jnp.stack([body[:, :, :64], body[:, :, 64:], shifted[:, :, 64:], shifted[:, :, :64]])
    got = lax.all_to_all(deal, "segment", split_axis=0, concat_axis=0, tiled=True)

    weight_sum = jnp.sum(seeing, axis=0)
    theta = pick(offset[..., 1], tile, 0).astype(F32) * (2.0 * jnp.pi / S)
    scal = jnp.stack([1.0 / weight_sum, jnp.cos(theta), jnp.sin(theta)], axis=1).reshape(-1)
    plain = seg < 2
    v = np.arange(S)
    eye = np.eye(S, dtype=np.float32)
    flip = jnp.where(plain, eye, eye[(-v) % S]).astype(BF)
    rot = jnp.where(plain, eye, eye[S - 1 - v]).astype(BF)
    small = np.eye(64, dtype=np.float32)
    lines = jnp.where(plain, small, small[::-1]).astype(BF)
    return finish(scal, got, flip, rot, lines)


def ramp_rows(taper, size):
    place = jnp.arange(size, dtype=jnp.float32)[None, :]
    width = taper.astype(jnp.float32)[:, None]
    left = jnp.where(place < width, 0.5 - 0.5 * jnp.cos(jnp.pi * (place + 0.5) / width), 1.0)
    return left * left[:, ::-1]


def dft_tables(size):
    steps = jnp.arange(size, dtype=jnp.int32)
    phase = steps[:, None] * steps[None, :] % size
    angle = 2.0 * jnp.pi * phase.astype(jnp.float32) / size
    factor = 1.0 / jnp.sqrt(jnp.float32(size))
    return (
        (jnp.cos(angle) * factor).astype(jnp.bfloat16),
        (jnp.sin(angle) * factor).astype(jnp.bfloat16),
    )


def first_pass(sub, cosine, sine):
    table = jnp.concatenate([cosine, -sine], axis=1)
    return jnp.einsum("fsxy,yk->fsxk", sub, table, preferred_element_type=jnp.float32).astype(
        jnp.bfloat16
    )


def second_pass(half, cosine, sine):
    size = cosine.shape[0]
    with_cos = jnp.einsum("ux,fsxk->fsuk", cosine, half, preferred_element_type=jnp.float32)
    with_sin = jnp.einsum("ux,fsxk->fsuk", sine, half, preferred_element_type=jnp.float32)
    real_part = with_cos[..., :size] + with_sin[..., size:]
    imag_part = with_cos[..., size:] - with_sin[..., :size]
    return (real_part, imag_part)


def local(raw_frames, dark_frame, flat_field, seeing, anchors, taper):
    size = S
    cosine, sine = dft_tables(size)
    ramps = ramp_rows(taper, size)
    calibrated = (
        raw_frames.astype(jnp.float32) - dark_frame.astype(jnp.float32)[None]
    ) / flat_field.astype(jnp.float32)[None]

    def cutout(anchor, ramp):
        start = jnp.zeros((), jnp.int32)
        cal = lax.dynamic_slice(
            calibrated, (start, anchor[0], anchor[1]), (calibrated.shape[0], size, size)
        )
        centered = cal - jnp.mean(cal, axis=(1, 2), keepdims=True)
        return (centered * (ramp[:, None] * ramp[None, :])[None]).astype(jnp.bfloat16)

    sub = jax.vmap(cutout, in_axes=(0, 0), out_axes=1)(anchors, ramps)
    received = lax.all_to_all(sub, "tile", split_axis=1, concat_axis=0, tiled=True)
    n_frames = received.shape[0]
    sub_dev = received.shape[1]
    block = math.gcd(n_frames, 8)
    n_blocks = n_frames // block
    segment_index = lax.axis_index("segment")
    weights = lax.dynamic_slice_in_dim(seeing, segment_index * n_frames, n_frames, 0)
    weight_sum = jnp.sum(seeing, axis=0)
    blocks = received.reshape((n_blocks, block) + received.shape[1:])
    weight_blocks = weights.reshape(n_blocks, block, sub_dev)

    def accumulate(carry, inputs):
        data, wblock = inputs
        half = first_pass(data, cosine, sine)
        real_part, imag_part = second_pass(half, cosine, sine)
        wgt = wblock[:, :, None, None]
        power_sum = carry[0] + jnp.sum(
            wgt * (real_part * real_part + imag_part * imag_part), axis=0
        )
        real_u = jnp.roll(real_part, -1, axis=2)
        imag_u = jnp.roll(imag_part, -1, axis=2)
        real_v = jnp.roll(real_part, -1, axis=3)
        imag_v = jnp.roll(imag_part, -1, axis=3)
        cross_sum = carry[1] + jnp.stack(
            [
                jnp.sum(wgt * (real_part * real_u + imag_part * imag_u), axis=0),
                jnp.sum(wgt * (imag_part * real_u - real_part * imag_u), axis=0),
                jnp.sum(wgt * (real_part * real_v + imag_part * imag_v), axis=0),
                jnp.sum(wgt * (imag_part * real_v - real_part * imag_v), axis=0),
            ],
            axis=1,
        )
        return ((power_sum, cross_sum), None)

    start_power = jnp.zeros((sub_dev, size, size), jnp.float32)
    start_cross = jnp.zeros((sub_dev, 4, size, size), jnp.float32)
    (power_sum, cross_sum), unused = lax.scan(
        accumulate, (start_power, start_cross), (blocks, weight_blocks)
    )
    power_rows, cross_rows = (
        lax.psum_scatter(
            power_sum.astype(jnp.bfloat16), "segment", scatter_dimension=1, tiled=True
        ).astype(jnp.float32),
        lax.psum_scatter(
            cross_sum.astype(jnp.bfloat16), "segment", scatter_dimension=2, tiled=True
        ).astype(jnp.float32),
    )
    power = power_rows / weight_sum[:, None, None]
    cross = cross_rows / weight_sum[:, None, None, None]
    return (power, cross)


def solution(mesh):
    placed = (P(("segment", "tile"), None, None), P(), P(), P(None, "tile"), P(), P())
    fits = mesh.shape["segment"] == 4 and mesh.shape["tile"] == 8

    def run(raw_frames, *rest):
        return (planes if fits and raw_frames.shape == (1, 1280, 1280) else local)(raw_frames, *rest)

    return jax.shard_map(
        run,
        mesh=mesh,
        in_specs=placed,
        out_specs=(P("tile", "segment", None), P("tile", None, "segment", None)),
        check_vma=False,
    )
```
